32 devices in a mesh: qrow: 8 (over z, x), kcol: 4 (over y, core).
Axes of the slice: x: 2, y: 2, z: 4, core: 2. Of those that a mesh axis runs over, the one named last changes fastest.
Arguments:
- queries: bfloat16 [128, 8192], P(('qrow', 'kcol')), may hold values from -200 to 200
- keys_values: bfloat16 [2, 4096, 512], P(None, ('kcol', 'qrow')), may hold values from -8 to 8
- doc_blocks: int32 [32], replicated, may hold values from 0 to 1, never falling along the last dimension, each value on 1 to 17 neighbouring positions
Outputs:
- attended: bfloat16 [128, 8192], P(('qrow', 'kcol'))
The draws below stay inside these ranges and needn't reach their ends.
Inputs may be any that keep to these rules, and one draw needn't show every extreme that they name: doc_blocks[b] is the document of positions 128 b to 128 b + 127; each document covers 1 to 17 consecutive entries (blocks), one document exactly that many.
All inputs are finite; a program needn't handle non-finite values.
Results may differ from the reference program's by a relative error of at most 0.0046.
Values may be sent and summed in bfloat16 or wider, within the bound.
A program may use at most 128 MiB of HBM per device.

```python
import math
import jax
import jax.numpy as jnp
import numpy as np
from jax import lax

QUERY_HEADS = 64
KEY_VALUE_HEADS = 4
HEAD_WIDTH = 128
TQ = 128
TOTAL_KEY_COUNT = 4096
STRIPE = 4096
KBLK = 32
DOCS = 2
N_KCOL = 4


def base_keys(key):
    return jax.random.truncated_normal(jax.random.fold_in(key, 11), -6.0, 6.0, (TOTAL_KEY_COUNT, KEY_VALUE_HEADS * HEAD_WIDTH), jnp.float32)


def draw_queries(key, part):
    shape_all = (TQ, QUERY_HEADS * HEAD_WIDTH)
    return jax.random.truncated_normal(jax.random.fold_in(key, 23), -6.0, 6.0, shape_all, jnp.float32).astype(jnp.bfloat16)


def draw_keys_values(key, part):
    key_matrix_rows = base_keys(key)
    value_matrix_rows = jax.random.truncated_normal(jax.random.fold_in(key, 37), -6.0, 6.0, (TOTAL_KEY_COUNT, KEY_VALUE_HEADS * HEAD_WIDTH), jnp.float32)
    return jnp.stack([key_matrix_rows, value_matrix_rows]).astype(jnp.bfloat16)


def split_up(amount, total, reach, slope):
    loads = [(1 << 20) // math.isqrt(grade ** slope) + 1 for grade in range(2, amount + 1)]
    surplus, counts = total - reach - (amount - 1), [1] * (amount - 1)
    while surplus > 0:
        candidates = [i for i in range(amount - 1) if counts[i] < reach]
        whole, left = sum([loads[i] for i in candidates]), surplus
        for i in candidates:
            addition = min(reach - counts[i], max(1, left * loads[i] // whole), surplus)
            counts[i] = counts[i] + addition
            surplus = surplus - addition
    return np.array([reach] + counts)


def ragged(own_key, amount, total, most, lean):
    if amount == 2:
        one = jax.random.randint(own_key, (), max(1, total - most), min(most, total - 1) + 1)
        return jnp.stack([one, total - one])
    tallies = jnp.asarray(split_up(amount, total, most, lean), jnp.int32)
    pairs = (amount - 1) // 2
    giver, sink = tallies[1:1 + 2 * pairs:2], tallies[2:2 + 2 * pairs:2]
    margin = jnp.minimum(giver - 1, most - sink)
    moved = jax.random.randint(jax.random.fold_in(own_key, 1), (pairs,), 0, 1 << 20) % (margin + 1)
    tallies = tallies.at[1:1 + 2 * pairs:2].set(giver - moved).at[2:2 + 2 * pairs:2].set(sink + moved)
    return tallies[jax.random.permutation(jax.random.fold_in(own_key, 2), amount)]


def setup_inputs(seed: int = 0) -> dict:
    key_of = jax.random.split(jax.random.key(seed), 4)
    queries = draw_queries(jax.random.fold_in(key_of[3], 71), 0)
    keys_values = draw_keys_values(jax.random.fold_in(key_of[3], 71), 0)
    doc_blocks = jnp.searchsorted(jnp.cumsum(ragged(key_of[2], DOCS, KBLK, KBLK // 2 + 1, 2)), jnp.arange(KBLK), side="right").astype(jnp.int32)
    return {"queries": queries, "keys_values": keys_values, "doc_blocks": doc_blocks}


masked_score = -1e+30

def reference(queries, keys_values, doc_blocks):
    query_group_width = QUERY_HEADS // KEY_VALUE_HEADS
    range_keys = TOTAL_KEY_COUNT // N_KCOL
    score_scale = 1.0 / math.sqrt(HEAD_WIDTH)
    key_pos = jnp.arange(TOTAL_KEY_COUNT, dtype=jnp.int32)
    key_doc = jnp.repeat(doc_blocks, 128)
    key_matrix_rows = keys_values[0].astype(jnp.float32)
    value_matrix_rows = keys_values[1].astype(jnp.float32)

    def one_block(block_index):
        block_index = block_index.astype(jnp.int32)
        first_row = block_index * 128
        query_rows = lax.dynamic_slice_in_dim(queries, first_row, 128, 0).astype(jnp.float32)
        query_pos = block_index * STRIPE + STRIPE - 128 + jnp.arange(128, dtype=jnp.int32)
        query_doc = doc_blocks[block_index * (STRIPE // 128) + STRIPE // 128 - 1]
        live_mask = (key_doc[None, :] == query_doc) & (key_pos[None, :] <= query_pos[:, None])
        ranged_mask = live_mask.reshape(1, 128, N_KCOL, range_keys)
        head_outputs = []
        for query_head_group in range(KEY_VALUE_HEADS):
            grouped = query_rows[:, query_head_group * query_group_width * HEAD_WIDTH:(query_head_group + 1) * query_group_width * HEAD_WIDTH].reshape(128, query_group_width, HEAD_WIDTH)
            key_part = key_matrix_rows[:, query_head_group * HEAD_WIDTH:(query_head_group + 1) * HEAD_WIDTH]
            value_part = value_matrix_rows[:, query_head_group * HEAD_WIDTH:(query_head_group + 1) * HEAD_WIDTH].reshape(N_KCOL, range_keys, HEAD_WIDTH)
            scores = jnp.einsum('qhd,kd->hqk', grouped, key_part) * score_scale
            scores = jnp.where(live_mask[None], scores, masked_score).reshape(query_group_width, 128, N_KCOL, range_keys)
            range_max = lax.optimization_barrier(jnp.max(scores, axis=3))
            weights = jnp.where(ranged_mask, jnp.exp(scores - range_max[..., None]), 0.0)
            range_sum = lax.optimization_barrier(jnp.sum(weights, axis=3))
            rounded = lax.optimization_barrier(weights.astype(jnp.bfloat16)).astype(jnp.float32)
            range_out = jnp.einsum('hqrk,rkd->hqrd', rounded, value_part)
            overall = lax.optimization_barrier(jnp.max(range_max, axis=2))
            factor = jnp.exp(range_max - overall[..., None])
            total_out = lax.optimization_barrier(jnp.sum(range_out * factor[..., None], axis=2))
            total_sum = lax.optimization_barrier(jnp.sum(range_sum * factor, axis=2))
            head_outputs.append(total_out / total_sum[..., None])
        joined = jnp.concatenate(head_outputs, axis=0)
        return jnp.transpose(joined, (1, 0, 2)).reshape(128, QUERY_HEADS * HEAD_WIDTH).astype(jnp.bfloat16)
    blocks = lax.map(one_block, jnp.arange(TQ // 128, dtype=jnp.int32))
    return blocks.reshape(TQ, QUERY_HEADS * HEAD_WIDTH)
```

```python
import math

import jax
import jax.numpy as jnp
from jax import lax
from jax.experimental import pallas as pl
from jax.experimental.pallas import tpu as pltpu
from jax.sharding import PartitionSpec as P

QUERY_HEADS = 64
KEY_VALUE_HEADS = 4
HEAD_WIDTH = 128
BLOCK = 128
MESH = pl.DeviceIdType.MESH

masked_score = -1e30


def dot(a, b, dims):
    return lax.dot_general(a, b, (dims, ((), ())), preferred_element_type=jnp.float32)


def make_kernel(rows_n, cols_n, local_rows, blocks_n):
    fold = max(1, 8 // cols_n)
    groups = rows_n // fold
    members = fold * cols_n
    heads = QUERY_HEADS // members
    slice_rows = local_rows * heads
    chunk_rows = members * slice_rows
    devices = rows_n * cols_n
    total_queries = devices * local_rows
    query_blocks = total_queries // BLOCK
    stripe_blocks = blocks_n // query_blocks
    chunk_queries = members * local_rows
    assert BLOCK % chunk_queries == 0 and blocks_n == devices
    first_live = max(0, stripe_blocks - 1 - blocks_n // 2)
    block_of = lambda e, g: (e % cols_n) * rows_n + g * fold + e // cols_n
    spans = [[block_of(e, g) >= first_live for g in range(groups)] for e in range(members)]
    sure = [e for e in range(members) if all(spans[e])]
    maybe = [e for e in range(members) if any(spans[e]) and not all(spans[e])]
    slots = sure + maybe
    scale = 1.0 / math.sqrt(HEAD_WIDTH)

    def where_is(group, member):
        return (group * fold + member // cols_n, member % cols_n)

    def kernel(doc_ref, q_ref, kv_ref, out_ref, qbuf, kvbuf, osend, ssend, obuf, sbuf,
               q_send, q_recv, kv_send, kv_recv, o_send, o_recv, s_send, s_recv):
        row, col = lax.axis_index("qrow"), lax.axis_index("kcol")
        group = row // fold
        member = (row % fold) * cols_n + col
        me = row * cols_n + col
        my_block = col * rows_n + row
        my_slot = sum(i * (member == e).astype(jnp.int32) for i, e in enumerate(slots))

        barrier = pltpu.get_barrier_semaphore()

        @pl.loop(1, devices)
        def _(k):
            other = lax.rem(me + k, devices)
            pl.semaphore_signal(barrier, inc=1, device_id=(other // cols_n, other % cols_n), device_id_type=MESH)

        for i, e in enumerate(maybe):
            @pl.when(block_of(e, group) < first_live)
            def _():
                kvbuf[len(sure) + i] = jnp.zeros((2, BLOCK, HEAD_WIDTH), kvbuf.dtype)

        pl.semaphore_wait(barrier, devices - 1)

        def kv_part(e):
            first = pl.multiple_of(e * heads // (QUERY_HEADS // KEY_VALUE_HEADS) * HEAD_WIDTH, HEAD_WIDTH)
            return kv_ref.at[:, :, pl.ds(first, HEAD_WIDTH)]

        def kv_copy(k):
            e = lax.rem(member + k, members)
            return pltpu.make_async_remote_copy(
                src_ref=kv_part(e), dst_ref=kvbuf.at[my_slot], send_sem=kv_send.at[k],
                recv_sem=kv_recv.at[my_slot], device_id=where_is(group, e), device_id_type=MESH)

        @pl.when(my_block >= first_live)
        def _():
            pltpu.make_async_copy(kv_part(member), kvbuf.at[my_slot], kv_recv.at[my_slot]).start()
            for k in range(1, members):
                kv_copy(k).start()

        pltpu.make_async_copy(q_ref.at[member], qbuf.at[me], q_recv.at[group]).start()

        @pl.loop(1, devices)
        def _(k):
            other = lax.rem(me + k, devices)
            e = lax.rem(other, members)
            pltpu.make_async_remote_copy(
                src_ref=q_ref.at[e], dst_ref=qbuf.at[me], send_sem=q_send, recv_sem=q_recv.at[group],
                device_id=(other // cols_n, other % cols_n), device_id_type=MESH).start()

        for i, e in enumerate(slots):
            wait = pltpu.make_async_copy(kvbuf.at[i], kvbuf.at[i], kv_recv.at[i]).wait
            if e in sure:
                wait()
            else:
                pl.when(block_of(e, group) >= first_live)(wait)

        lane = lax.broadcasted_iota(jnp.int32, (chunk_rows, BLOCK), 1)
        row_index = lax.broadcasted_iota(jnp.int32, (chunk_rows, BLOCK), 0)
        row_query = row_index // heads
        diagonal = (lax.broadcasted_iota(jnp.int32, (slice_rows, BLOCK), 0)
                    == lax.broadcasted_iota(jnp.int32, (slice_rows, BLOCK), 1))

        def attend(source):
            first = source * members
            mine = qbuf.at[pl.ds(first, members)]
            pltpu.make_async_copy(mine, mine, q_recv.at[source]).wait()
            q = qbuf[pl.ds(first, members)].reshape(chunk_rows, HEAD_WIDTH)
            query_first = source * chunk_queries
            query_block = (query_first // BLOCK + 1) * stripe_blocks - 1
            in_block = row_query + query_first % BLOCK
            query_doc = doc_ref[query_block]
            scores = []
            for i, e in enumerate(slots):
                b = block_of(e, group)
                same = doc_ref[b] == query_doc
                whole = jnp.where(same & (b < query_block), BLOCK, -1)
                causal = jnp.where(same & (b == query_block), 0, -2 * BLOCK)
                limit = jnp.maximum(in_block + causal, whole)
                s = dot(q, kvbuf[i, 0], ((1,), (1,))) * scale
                scores.append((s, lane <= limit))
            masked = [jnp.where(live, s, masked_score) for s, live in scores]
            top = masked[0]
            for s in masked[1:]:
                top = jnp.maximum(top, s)
            top = jnp.max(top, axis=1, keepdims=True)
            total = None
            acc = None
            for i in range(len(slots)):
                p = jnp.where(scores[i][1], jnp.exp(masked[i] - top), 0.0)
                total = p if total is None else total + p
                o = dot(p.astype(jnp.bfloat16), kvbuf[i, 1], ((1,), (0,)))
                acc = o if acc is None else acc + o
            total = jnp.sum(total, axis=1, keepdims=True)
            osend[pl.ds(first, members)] = acc.astype(jnp.bfloat16).reshape(members, slice_rows, HEAD_WIDTH)
            for j in range(members):
                part = slice(j * slice_rows, (j + 1) * slice_rows)
                ssend[first + j, 0:1] = jnp.sum(jnp.where(diagonal, top[part], 0.0), axis=0, keepdims=True)
                ssend[first + j, 1:2] = jnp.sum(jnp.where(diagonal, total[part], 0.0), axis=0, keepdims=True)

        def give(source, j):
            k = source * members + j
            return [
                pltpu.make_async_remote_copy(
                    src_ref=src.at[k], dst_ref=dst.at[group, member], send_sem=sent, recv_sem=got.at[group],
                    device_id=where_is(source, j), device_id_type=MESH)
                for src, dst, sent, got in ((osend, obuf, o_send, o_recv), (ssend, sbuf, s_send, s_recv))
            ]

        attend(group)
        pltpu.make_async_copy(osend.at[me], obuf.at[group, member], o_recv.at[group]).start()
        pltpu.make_async_copy(ssend.at[me], sbuf.at[group, member], s_recv.at[group]).start()
        for i in range(1, members):
            for copy in give(group, lax.rem(member + i, members)):
                copy.start()

        @pl.loop(1, groups)
        def _(k):
            source = lax.rem(group + k, groups)
            attend(source)
            for j in range(members):
                for copy in give(source, j):
                    copy.start()

        for g in range(groups):
            pltpu.make_async_copy(sbuf.at[g], sbuf.at[g], s_recv.at[g]).wait()
            pltpu.make_async_copy(obuf.at[g], obuf.at[g], o_recv.at[g]).wait()

        for e in range(members):
            tops = [sbuf[g, e, 0:1] for g in range(groups)]
            overall = tops[0]
            for t in tops[1:]:
                overall = jnp.maximum(overall, t)
            factors = [jnp.exp(t - overall) for t in tops]
            weight = sum(f * sbuf[g, e, 1:2] for g, f in enumerate(factors))
            merged = None
            for g, f in enumerate(factors):
                column = jnp.sum(jnp.where(diagonal, f, 0.0), axis=1, keepdims=True)
                term = column * obuf[g, e].astype(jnp.float32)
                merged = term if merged is None else merged + term
            column = jnp.sum(jnp.where(diagonal, weight, 0.0), axis=1, keepdims=True)
            out_ref[e] = (merged / column).astype(out_ref.dtype)

        @pl.when(my_block >= first_live)
        def _():
            for k in range(1, members):
                kv_copy(k).wait_send()
        others = qbuf.at[pl.ds(0, devices - 1)]
        pltpu.make_async_copy(others, others, q_send).wait()
        others = osend.at[pl.ds(0, devices - 1)]
        pltpu.make_async_copy(others, others, o_send).wait()
        others = ssend.at[pl.ds(0, devices - 1)]
        pltpu.make_async_copy(others, others, s_send).wait()

    bf16, dma = jnp.bfloat16, pltpu.SemaphoreType.DMA
    scratch = [
        pltpu.VMEM((devices, slice_rows, HEAD_WIDTH), bf16),
        pltpu.VMEM((len(slots), 2, BLOCK, HEAD_WIDTH), bf16),
        pltpu.VMEM((devices, slice_rows, HEAD_WIDTH), bf16),
        pltpu.VMEM((devices, 2, BLOCK), jnp.float32),
        pltpu.VMEM((groups, members, slice_rows, HEAD_WIDTH), bf16),
        pltpu.VMEM((groups, members, 2, BLOCK), jnp.float32),
        dma, dma((groups,)), dma((members,)), dma((len(slots),)),
        dma, dma((groups,)), dma, dma((groups,)),
    ]
    return kernel, scratch, members, heads, slice_rows


def solution(mesh):
    rows_n, cols_n = mesh.shape["qrow"], mesh.shape["kcol"]

    def per_device(queries, keys_values, doc_blocks):
        local_rows = queries.shape[0]
        kernel, scratch, members, heads, slice_rows = make_kernel(rows_n, cols_n, local_rows, doc_blocks.shape[0])
        q = queries.reshape(local_rows, members, heads, HEAD_WIDTH).transpose(1, 0, 2, 3)
        q = q.reshape(members, slice_rows, HEAD_WIDTH)
        out = pl.pallas_call(
            kernel,
            out_shape=jax.ShapeDtypeStruct((members, slice_rows, HEAD_WIDTH), jnp.bfloat16),
            in_specs=[
                pl.BlockSpec(memory_space=pltpu.SMEM),
                pl.BlockSpec(memory_space=pl.ANY),
                pl.BlockSpec(memory_space=pl.ANY),
            ],
            out_specs=pl.BlockSpec(memory_space=pltpu.VMEM),
            scratch_shapes=scratch,
            compiler_params=pltpu.CompilerParams(collective_id=0, has_side_effects=True),
        )(doc_blocks, q, keys_values)
        out = out.reshape(members, local_rows, heads, HEAD_WIDTH).transpose(1, 0, 2, 3)
        return out.reshape(local_rows, QUERY_HEADS * HEAD_WIDTH)

    return jax.shard_map(
        per_device,
        mesh=mesh,
        in_specs=(P(("qrow", "kcol"), None), P(None, ("kcol", "qrow"), None), P()),
        out_specs=P(("qrow", "kcol"), None),
        check_vma=False,
    )
```

```python
import math

import jax
import jax.numpy as jnp
from jax import lax
from jax.experimental import pallas as pl
from jax.experimental.pallas import tpu as pltpu
from jax.sharding import PartitionSpec as P

QUERY_HEADS = 64
KEY_VALUE_HEADS = 4
HEAD_WIDTH = 128
BLOCK = 128
MESH = pl.DeviceIdType.MESH

masked_score = -1e30


def dot(a, b, dims):
    return lax.dot_general(a, b, (dims, ((), ())), preferred_element_type=jnp.float32)


def make_kernel(rows_n, cols_n, local_rows, blocks_n):
    fold = max(1, 8 // cols_n)
    groups = rows_n // fold
    members = fold * cols_n
    heads = QUERY_HEADS // members
    slice_rows = local_rows * heads
    chunk_rows = members * slice_rows
    devices = rows_n * cols_n
    total_queries = devices * local_rows
    query_blocks = total_queries // BLOCK
    stripe_blocks = blocks_n // query_blocks
    chunk_queries = members * local_rows
    assert BLOCK % chunk_queries == 0 and blocks_n == devices and cols_n % 2 == 0 and 2 * slice_rows <= BLOCK
    first_live = max(0, stripe_blocks - 1 - blocks_n // 2)
    block_of = lambda e, g: (e % cols_n) * rows_n + g * fold + e // cols_n
    spans = [[block_of(e, g) >= first_live for g in range(groups)] for e in range(members)]
    sure = [e for e in range(members) if all(spans[e])]
    maybe = [e for e in range(members) if any(spans[e]) and not all(spans[e])]
    slots = sure + maybe
    scale = 1.0 / math.sqrt(HEAD_WIDTH)

    def where_is(group, member):
        return (group * fold + member // cols_n, member % cols_n)

    def kernel(doc_ref, q_ref, kv_ref, out_ref, qsend, wide, qbuf, kvbuf, osend, ssend, obuf, sbuf,
               q_send, q_recv, kv_send, kv_recv, pair_send, pair_recv, o_send, o_recv, s_send, s_recv):
        row, col = lax.axis_index("qrow"), lax.axis_index("kcol")
        group = row // fold
        member = (row % fold) * cols_n + col
        me = row * cols_n + col
        my_block = col * rows_n + row
        my_slot = sum(i * (member == e).astype(jnp.int32) for i, e in enumerate(slots))

        half = lax.rem(member, 2)
        barrier = pltpu.get_barrier_semaphore()

        @pl.loop(1, devices)
        def _(k):
            other = lax.rem(me + k, devices)
            pl.semaphore_signal(barrier, inc=1, device_id=(other // cols_n, other % cols_n), device_id_type=MESH)

        for i, e in enumerate(maybe):
            @pl.when(block_of(e, group) < first_live)
            def _():
                kvbuf[len(sure) + i] = jnp.zeros((2, BLOCK, HEAD_WIDTH), kvbuf.dtype)

        for e in range(members):
            for h in range(heads):
                first = (e * heads + h) * HEAD_WIDTH
                wide[e, h * local_rows:(h + 1) * local_rows] = q_ref[:, first:first + HEAD_WIDTH].astype(jnp.float32)
            qsend[e] = wide[e].astype(qsend.dtype)

        pl.semaphore_wait(barrier, devices - 1)

        def kv_part(e):
            first = pl.multiple_of(e * heads // (QUERY_HEADS // KEY_VALUE_HEADS) * HEAD_WIDTH, HEAD_WIDTH)
            return kv_ref.at[lax.rem(e, 2), :, pl.ds(first, HEAD_WIDTH)]

        def kv_copy(k):
            e = lax.rem(member + k, members)
            return pltpu.make_async_remote_copy(
                src_ref=kv_part(e), dst_ref=kvbuf.at[my_slot, lax.rem(e, 2)], send_sem=kv_send.at[k],
                recv_sem=kv_recv.at[my_slot], device_id=where_is(group, e), device_id_type=MESH)

        @pl.when(my_block >= first_live)
        def _():
            pltpu.make_async_copy(kv_part(member), kvbuf.at[my_slot, half], kv_recv.at[my_slot]).start()
            for k in range(1, members):
                kv_copy(k).start()

        pltpu.make_async_copy(qsend.at[member], qbuf.at[me], q_recv.at[group]).start()

        @pl.loop(1, devices)
        def _(k):
            other = lax.rem(me + k, devices)
            e = lax.rem(other, members)
            pltpu.make_async_remote_copy(
                src_ref=qsend.at[e], dst_ref=qbuf.at[me], send_sem=q_send, recv_sem=q_recv.at[group],
                device_id=(other // cols_n, other % cols_n), device_id_type=MESH).start()

        def pair_copy(i):
            return pltpu.make_async_remote_copy(
                src_ref=kvbuf.at[i, half], dst_ref=kvbuf.at[i, half], send_sem=pair_send.at[i],
                recv_sem=pair_recv.at[i], device_id=(row, col + 1 - 2 * lax.rem(col, 2)), device_id_type=MESH)

        def per_slot(step):
            for i, e in enumerate(slots):
                if e in sure:
                    step(i)
                else:
                    pl.when(block_of(e, group) >= first_live)(lambda: step(i))

        def pass_on(i):
            pltpu.make_async_copy(kvbuf.at[i, half], kvbuf.at[i, half], kv_recv.at[i]).wait()
            pair_copy(i).start()

        per_slot(pass_on)
        per_slot(lambda i: pair_copy(i).wait_recv())

        lane = lax.broadcasted_iota(jnp.int32, (chunk_rows, BLOCK), 1)
        row_index = lax.broadcasted_iota(jnp.int32, (chunk_rows, BLOCK), 0)
        row_query = row_index // slice_rows * local_rows + row_index % local_rows
        offset = (lax.broadcasted_iota(jnp.int32, (slice_rows, BLOCK), 1)
                  - lax.broadcasted_iota(jnp.int32, (slice_rows, BLOCK), 0))
        top_place, total_place = offset == 0, offset == slice_rows

        def attend(source):
            first = source * members
            mine = qbuf.at[pl.ds(first, members)]
            pltpu.make_async_copy(mine, mine, q_recv.at[source]).wait()
            q = qbuf[pl.ds(first, members)].reshape(chunk_rows, HEAD_WIDTH)
            query_first = source * chunk_queries
            query_block = (query_first // BLOCK + 1) * stripe_blocks - 1
            in_block = row_query + query_first % BLOCK
            query_doc = doc_ref[query_block]
            scores = []
            for i, e in enumerate(slots):
                b = block_of(e, group)
                same = doc_ref[b] == query_doc
                whole = jnp.where(same & (b < query_block), BLOCK, -1)
                causal = jnp.where(same & (b == query_block), 0, -2 * BLOCK)
                limit = jnp.maximum(in_block + causal, whole)
                s = dot(q, kvbuf[i, 0], ((1,), (1,))) * scale
                scores.append((s, lane <= limit))
            masked = [jnp.where(live, s, masked_score) for s, live in scores]
            top = masked[0]
            for s in masked[1:]:
                top = jnp.maximum(top, s)
            top = jnp.max(top, axis=1, keepdims=True)
            total = None
            acc = None
            for i in range(len(slots)):
                p = jnp.where(scores[i][1], jnp.exp(masked[i] - top), 0.0)
                total = p if total is None else total + p
                o = dot(p.astype(jnp.bfloat16), kvbuf[i, 1], ((1,), (0,)))
                acc = o if acc is None else acc + o
            total = jnp.sum(total, axis=1, keepdims=True)
            osend[pl.ds(first, members)] = acc.astype(jnp.bfloat16).reshape(members, slice_rows, HEAD_WIDTH)
            for j in range(members):
                part = slice(j * slice_rows, (j + 1) * slice_rows)
                stats = jnp.where(top_place, top[part], jnp.where(total_place, total[part], 0.0))
                ssend[first + j] = jnp.sum(stats, axis=0, keepdims=True)

        def give(source, j):
            k = source * members + j
            return [
                pltpu.make_async_remote_copy(
                    src_ref=src.at[k], dst_ref=dst.at[group, member], send_sem=sent, recv_sem=got.at[group],
                    device_id=where_is(source, j), device_id_type=MESH)
                for src, dst, sent, got in ((osend, obuf, o_send, o_recv), (ssend, sbuf, s_send, s_recv))
            ]

        attend(group)
        pltpu.make_async_copy(osend.at[me], obuf.at[group, member], o_recv.at[group]).start()
        pltpu.make_async_copy(ssend.at[me], sbuf.at[group, member], s_recv.at[group]).start()
        for i in range(1, members):
            for copy in give(group, lax.rem(member + i, members)):
                copy.start()

        @pl.loop(1, groups)
        def _(k):
            source = lax.rem(group + k, groups)
            attend(source)
            for j in range(members):
                for copy in give(source, j):
                    copy.start()

        for g in range(groups):
            pltpu.make_async_copy(sbuf.at[g], sbuf.at[g], s_recv.at[g]).wait()
            pltpu.make_async_copy(obuf.at[g], obuf.at[g], o_recv.at[g]).wait()

        for e in range(members):
            column = lambda g, place: jnp.sum(jnp.where(place, sbuf[g, e], 0.0), axis=1, keepdims=True)
            tops = [column(g, top_place) for g in range(groups)]
            overall = tops[0]
            for t in tops[1:]:
                overall = jnp.maximum(overall, t)
            merged = weight = None
            for g in range(groups):
                factor = jnp.exp(tops[g] - overall)
                term = factor * obuf[g, e].astype(jnp.float32)
                part = factor * column(g, total_place)
                merged = term if merged is None else merged + term
                weight = part if weight is None else weight + part
            wide[e] = merged / weight
            for h in range(heads):
                first = (e * heads + h) * HEAD_WIDTH
                out_ref[:, first:first + HEAD_WIDTH] = wide[e, h * local_rows:(h + 1) * local_rows].astype(out_ref.dtype)

        per_slot(lambda i: pair_copy(i).wait_send())

        @pl.when(my_block >= first_live)
        def _():
            for k in range(1, members):
                kv_copy(k).wait_send()
        others = qbuf.at[pl.ds(0, devices - 1)]
        pltpu.make_async_copy(others, others, q_send).wait()
        others = osend.at[pl.ds(0, devices - 1)]
        pltpu.make_async_copy(others, others, o_send).wait()
        others = ssend.at[pl.ds(0, devices - 1)]
        pltpu.make_async_copy(others, others, s_send).wait()

    bf16, dma = jnp.bfloat16, pltpu.SemaphoreType.DMA
    scratch = [
        pltpu.VMEM((members, slice_rows, HEAD_WIDTH), bf16),
        pltpu.VMEM((members, slice_rows, HEAD_WIDTH), jnp.float32),
        pltpu.VMEM((devices, slice_rows, HEAD_WIDTH), bf16),
        pltpu.VMEM((len(slots), 2, BLOCK, HEAD_WIDTH), bf16),
        pltpu.VMEM((devices, slice_rows, HEAD_WIDTH), bf16),
        pltpu.VMEM((devices, 1, BLOCK), jnp.float32),
        pltpu.VMEM((groups, members, slice_rows, HEAD_WIDTH), bf16),
        pltpu.VMEM((groups, members, 1, BLOCK), jnp.float32),
        dma, dma((groups,)), dma((members,)), dma((len(slots),)), dma((len(slots),)), dma((len(slots),)),
        dma, dma((groups,)), dma, dma((groups,)),
    ]
    return kernel, scratch


def solution(mesh):
    rows_n, cols_n = mesh.shape["qrow"], mesh.shape["kcol"]

    def per_device(queries, keys_values, doc_blocks):
        local_rows = queries.shape[0]
        kernel, scratch = make_kernel(rows_n, cols_n, queries.shape[0], doc_blocks.shape[0])
        return pl.pallas_call(
            kernel,
            out_shape=jax.ShapeDtypeStruct(queries.shape, queries.dtype),
            in_specs=[
                pl.BlockSpec(memory_space=pltpu.SMEM),
                pl.BlockSpec(memory_space=pltpu.VMEM),
                pl.BlockSpec(memory_space=pl.ANY),
            ],
            out_specs=pl.BlockSpec(memory_space=pltpu.VMEM),
            scratch_shapes=scratch,
            compiler_params=pltpu.CompilerParams(collective_id=0, has_side_effects=True),
        )(doc_blocks, queries, keys_values)

    return jax.shard_map(
        per_device,
        mesh=mesh,
        in_specs=(P(("qrow", "kcol"), None), P(None, ("kcol", "qrow"), None), P()),
        out_specs=P(("qrow", "kcol"), None),
        check_vma=False,
    )
```

```python
import math

import jax
import jax.numpy as jnp
from jax import lax
from jax.experimental import pallas as pl
from jax.experimental.pallas import tpu as pltpu
from jax.sharding import PartitionSpec as P

QUERY_HEADS = 64
KEY_VALUE_HEADS = 4
HEAD_WIDTH = 128
BLOCK = 128
MESH = pl.DeviceIdType.MESH

masked_score = -1e30


def dot(a, b, dims):
    return lax.dot_general(a, b, (dims, ((), ())), preferred_element_type=jnp.float32)


def make_kernel(rows_n, cols_n, local_rows, blocks_n):
    fold = max(1, 8 // cols_n)
    groups = rows_n // fold
    members = fold * cols_n
    heads = QUERY_HEADS // members
    slice_rows = local_rows * heads
    chunk_rows = members * slice_rows
    devices = rows_n * cols_n
    total_queries = devices * local_rows
    query_blocks = total_queries // BLOCK
    stripe_blocks = blocks_n // query_blocks
    chunk_queries = members * local_rows
    assert BLOCK % chunk_queries == 0 and blocks_n == devices and cols_n % 2 == 0 and 2 * slice_rows <= BLOCK
    first_live = max(0, stripe_blocks - 1 - blocks_n // 2)
    block_of = lambda e, g: (e % cols_n) * rows_n + g * fold + e // cols_n
    spans = [[block_of(e, g) >= first_live for g in range(groups)] for e in range(members)]
    sure = [e for e in range(members) if all(spans[e])]
    maybe = [e for e in range(members) if any(spans[e]) and not all(spans[e])]
    slots = sure + maybe
    scale = math.log2(math.e) / math.sqrt(HEAD_WIDTH)

    apart = max(1, groups // 2)

    def visited(group, k):
        block = group // apart
        far = lax.rem(block + 1, groups // apart) * apart + lax.rem(group + k, apart)
        near = block * apart + lax.rem(group + k - apart, apart)
        return jnp.where(k == 0, group, jnp.where(k <= apart, far, near))

    def where_is(group, member):
        return (group * fold + member // cols_n, member % cols_n)

    def kernel(doc_ref, q_ref, kv_ref, out_ref, local, local_sem, qsend, wide, qbuf, kvbuf, osend, ssend, obuf, sbuf,
               q_send, q_recv, kv_send, kv_recv, pair_send, pair_recv, o_send, o_recv, s_send, s_recv):
        row, col = lax.axis_index("qrow"), lax.axis_index("kcol")
        group = row // fold
        member = (row % fold) * cols_n + col
        me = row * cols_n + col
        my_block = col * rows_n + row
        my_slot = sum(i * (member == e).astype(jnp.int32) for i, e in enumerate(slots))

        half = lax.rem(member, 2)
        barrier = pltpu.get_barrier_semaphore()

        fetch = pltpu.make_async_copy(kv_ref, local, local_sem)
        fetch.start()

        @pl.loop(1, devices)
        def _(k):
            other = lax.rem(me + k, devices)
            pl.semaphore_signal(barrier, inc=1, device_id=(other // cols_n, other % cols_n), device_id_type=MESH)

        for i, e in enumerate(maybe):
            @pl.when(block_of(e, group) < first_live)
            def _():
                kvbuf[:, len(sure) + i] = jnp.zeros((2, BLOCK, HEAD_WIDTH), kvbuf.dtype)

        for e in range(members):
            for h in range(heads):
                first = (e * heads + h) * HEAD_WIDTH
                wide[e, h * local_rows:(h + 1) * local_rows] = q_ref[:, first:first + HEAD_WIDTH].astype(jnp.float32)
            qsend[e] = wide[e].astype(qsend.dtype)

        fetch.wait()
        pl.semaphore_wait(barrier, devices - 1)

        def kv_part(e):
            first = pl.multiple_of(e * heads // (QUERY_HEADS // KEY_VALUE_HEADS) * HEAD_WIDTH, HEAD_WIDTH)
            return local.at[lax.rem(e, 2), :, pl.ds(first, HEAD_WIDTH)]

        def kv_copy(k):
            e = lax.rem(member + k, members)
            return pltpu.make_async_remote_copy(
                src_ref=kv_part(e), dst_ref=kvbuf.at[lax.rem(e, 2), my_slot], send_sem=kv_send.at[k],
                recv_sem=kv_recv.at[my_slot], device_id=where_is(group, e), device_id_type=MESH)

        @pl.when(my_block >= first_live)
        def _():
            pltpu.make_async_copy(kv_part(member), kvbuf.at[half, my_slot], kv_recv.at[my_slot]).start()
            for k in range(1, members):
                kv_copy(k).start()

        pltpu.make_async_copy(qsend.at[member], qbuf.at[me], q_recv.at[group]).start()

        @pl.loop(1, devices)
        def _(k):
            e = lax.rem(member + k, members)
            pltpu.make_async_remote_copy(
                src_ref=qsend.at[e], dst_ref=qbuf.at[me], send_sem=q_send, recv_sem=q_recv.at[group],
                device_id=where_is(visited(group, k // members), e), device_id_type=MESH).start()

        def pair_copy(i):
            return pltpu.make_async_remote_copy(
                src_ref=kvbuf.at[half, i], dst_ref=kvbuf.at[half, i], send_sem=pair_send.at[i],
                recv_sem=pair_recv.at[i], device_id=(row, col + 1 - 2 * lax.rem(col, 2)), device_id_type=MESH)

        def per_slot(step):
            for i, e in enumerate(slots):
                if e in sure:
                    step(i)
                else:
                    pl.when(block_of(e, group) >= first_live)(lambda: step(i))

        def pass_on(i):
            pltpu.make_async_copy(kvbuf.at[half, i], kvbuf.at[half, i], kv_recv.at[i]).wait()
            pair_copy(i).start()

        per_slot(pass_on)
        per_slot(lambda i: pair_copy(i).wait_recv())

        lane = lax.broadcasted_iota(jnp.int32, (chunk_rows, BLOCK), 1)
        row_index = lax.broadcasted_iota(jnp.int32, (chunk_rows, BLOCK), 0)
        row_query = row_index // slice_rows * local_rows + row_index % local_rows
        offset = (lax.broadcasted_iota(jnp.int32, (slice_rows, BLOCK), 1)
                  - lax.broadcasted_iota(jnp.int32, (slice_rows, BLOCK), 0))
        top_place, total_place = offset == 0, offset == slice_rows

        def attend(source):
            first = source * members
            mine = qbuf.at[pl.ds(first, members)]
            pltpu.make_async_copy(mine, mine, q_recv.at[source]).wait()
            q = qbuf[pl.ds(first, members)].reshape(chunk_rows, HEAD_WIDTH)
            query_first = source * chunk_queries
            query_block = (query_first // BLOCK + 1) * stripe_blocks - 1
            in_block = row_query + query_first % BLOCK
            query_doc = doc_ref[query_block]
            keys = kvbuf[0].reshape(len(slots) * BLOCK, HEAD_WIDTH)
            values = kvbuf[1].reshape(len(slots) * BLOCK, HEAD_WIDTH)
            scores = dot(q, keys, ((1,), (1,)))
            masked = []
            for i, e in enumerate(slots):
                b = block_of(e, group)
                same = doc_ref[b] == query_doc
                whole = jnp.where(same & (b < query_block), BLOCK, -1)
                causal = jnp.where(same & (b == query_block), 0, -2 * BLOCK)
                limit = jnp.maximum(in_block + causal, whole)
                masked.append(jnp.where(lane <= limit, scores[:, i * BLOCK:(i + 1) * BLOCK], masked_score))
            top = masked[0]
            for s in masked[1:]:
                top = jnp.maximum(top, s)
            top = jnp.maximum(jnp.max(top, axis=1, keepdims=True), 0.5 * masked_score)
            weights = [jnp.exp2((s - top) * scale) for s in masked]
            total = weights[0]
            for p in weights[1:]:
                total = total + p
            total = jnp.sum(total, axis=1, keepdims=True)
            acc = dot(jnp.concatenate([p.astype(jnp.bfloat16) for p in weights], axis=1), values, ((1,), (0,)))
            osend[pl.ds(first, members)] = acc.astype(jnp.bfloat16).reshape(members, slice_rows, HEAD_WIDTH)
            for j in range(members):
                part = slice(j * slice_rows, (j + 1) * slice_rows)
                stats = jnp.where(top_place, top[part], jnp.where(total_place, total[part], 0.0))
                ssend[first + j] = jnp.sum(stats, axis=0, keepdims=True)

        def give(source, j):
            k = source * members + j
            return [
                pltpu.make_async_remote_copy(
                    src_ref=src.at[k], dst_ref=dst.at[group, member], send_sem=sent, recv_sem=got.at[group],
                    device_id=where_is(source, j), device_id_type=MESH)
                for src, dst, sent, got in ((osend, obuf, o_send, o_recv), (ssend, sbuf, s_send, s_recv))
            ]

        attend(group)
        pltpu.make_async_copy(osend.at[me], obuf.at[group, member], o_recv.at[group]).start()
        pltpu.make_async_copy(ssend.at[me], sbuf.at[group, member], s_recv.at[group]).start()
        for i in range(1, members):
            for copy in give(group, lax.rem(member + i, members)):
                copy.start()

        @pl.loop(1, groups)
        def _(k):
            source = lax.rem(group + k, groups)
            attend(source)
            for j in range(members):
                for copy in give(source, j):
                    copy.start()

        for g in range(groups):
            pltpu.make_async_copy(sbuf.at[g], sbuf.at[g], s_recv.at[g]).wait()
            pltpu.make_async_copy(obuf.at[g], obuf.at[g], o_recv.at[g]).wait()

        for e in range(members):
            column = lambda g, place: jnp.sum(jnp.where(place, sbuf[g, e], 0.0), axis=1, keepdims=True)
            tops = [column(g, top_place) for g in range(groups)]
            overall = tops[0]
            for t in tops[1:]:
                overall = jnp.maximum(overall, t)
            merged = weight = None
            for g in range(groups):
                factor = jnp.exp2((tops[g] - overall) * scale)
                term = factor * obuf[g, e].astype(jnp.float32)
                part = factor * column(g, total_place)
                merged = term if merged is None else merged + term
                weight = part if weight is None else weight + part
            wide[e] = merged / weight
            for h in range(heads):
                first = (e * heads + h) * HEAD_WIDTH
                out_ref[:, first:first + HEAD_WIDTH] = wide[e, h * local_rows:(h + 1) * local_rows].astype(out_ref.dtype)

        per_slot(lambda i: pair_copy(i).wait_send())

        @pl.when(my_block >= first_live)
        def _():
            for k in range(1, members):
                kv_copy(k).wait_send()
        others = qbuf.at[pl.ds(0, devices - 1)]
        pltpu.make_async_copy(others, others, q_send).wait()
        others = osend.at[pl.ds(0, devices - 1)]
        pltpu.make_async_copy(others, others, o_send).wait()
        others = ssend.at[pl.ds(0, devices - 1)]
        pltpu.make_async_copy(others, others, s_send).wait()

    bf16, dma = jnp.bfloat16, pltpu.SemaphoreType.DMA
    scratch = [
        pltpu.VMEM((2, BLOCK, KEY_VALUE_HEADS * HEAD_WIDTH), bf16),
        dma,
        pltpu.VMEM((members, slice_rows, HEAD_WIDTH), bf16),
        pltpu.VMEM((members, slice_rows, HEAD_WIDTH), jnp.float32),
        pltpu.VMEM((devices, slice_rows, HEAD_WIDTH), bf16),
        pltpu.VMEM((2, len(slots), BLOCK, HEAD_WIDTH), bf16),
        pltpu.VMEM((devices, slice_rows, HEAD_WIDTH), bf16),
        pltpu.VMEM((devices, 1, BLOCK), jnp.float32),
        pltpu.VMEM((groups, members, slice_rows, HEAD_WIDTH), bf16),
        pltpu.VMEM((groups, members, 1, BLOCK), jnp.float32),
        dma, dma((groups,)), dma((members,)), dma((len(slots),)), dma((len(slots),)), dma((len(slots),)),
        dma, dma((groups,)), dma, dma((groups,)),
    ]
    return kernel, scratch


def solution(mesh):
    rows_n, cols_n = mesh.shape["qrow"], mesh.shape["kcol"]

    def per_device(queries, keys_values, doc_blocks):
        local_rows = queries.shape[0]
        kernel, scratch = make_kernel(rows_n, cols_n, queries.shape[0], doc_blocks.shape[0])
        return pl.pallas_call(
            kernel,
            out_shape=jax.ShapeDtypeStruct(queries.shape, queries.dtype),
            in_specs=[
                pl.BlockSpec(memory_space=pltpu.SMEM),
                pl.BlockSpec(memory_space=pltpu.VMEM),
                pl.BlockSpec(memory_space=pl.ANY),
            ],
            out_specs=pl.BlockSpec(memory_space=pltpu.VMEM),
            scratch_shapes=scratch,
            compiler_params=pltpu.CompilerParams(collective_id=0, has_side_effects=True),
        )(doc_blocks, queries, keys_values)

    return jax.shard_map(
        per_device,
        mesh=mesh,
        in_specs=(P(("qrow", "kcol"), None), P(None, ("kcol", "qrow"), None), P()),
        out_specs=P(("qrow", "kcol"), None),
        check_vma=False,
    )
```

```python
import math

import jax
import jax.numpy as jnp
from jax import lax
from jax.experimental import pallas as pl
from jax.experimental.pallas import tpu as pltpu
from jax.sharding import PartitionSpec as P

QUERY_HEADS = 64
KEY_VALUE_HEADS = 4
HEAD_WIDTH = 128
BLOCK = 128
MESH = pl.DeviceIdType.MESH

masked_score = -1e30


def dot(a, b, dims):
    return lax.dot_general(a, b, (dims, ((), ())), preferred_element_type=jnp.float32)


def make_kernel(rows_n, cols_n, local_rows, blocks_n):
    fold = max(1, 8 // cols_n)
    groups = rows_n // fold
    members = fold * cols_n
    heads = QUERY_HEADS // members
    slice_rows = local_rows * heads
    chunk_rows = members * slice_rows
    devices = rows_n * cols_n
    total_queries = devices * local_rows
    query_blocks = total_queries // BLOCK
    stripe_blocks = blocks_n // query_blocks
    chunk_queries = members * local_rows
    assert BLOCK % chunk_queries == 0 and blocks_n == devices and cols_n % 2 == 0 and 2 * slice_rows <= BLOCK
    first_live = max(0, stripe_blocks - 1 - blocks_n // 2)
    block_of = lambda e, g: (e % cols_n) * rows_n + g * fold + e // cols_n
    spans = [[block_of(e, g) >= first_live for g in range(groups)] for e in range(members)]
    sure = [e for e in range(members) if all(spans[e])]
    maybe = [e for e in range(members) if any(spans[e]) and not all(spans[e])]
    slots = sure + maybe
    scale = math.log2(math.e) / math.sqrt(HEAD_WIDTH)

    apart = max(1, groups // 2)

    def visited(group, k):
        block = group // apart
        far = lax.rem(block + 1, groups // apart) * apart + lax.rem(group + k, apart)
        near = block * apart + lax.rem(group + k - apart, apart)
        return jnp.where(k == 0, group, jnp.where(k <= apart, far, near))

    def where_is(group, member):
        return (group * fold + member // cols_n, member % cols_n)

    def kernel(doc_ref, q_ref, kv_ref, out_ref, local, local_sem, qsend, wide, qbuf, kvbuf, osend, ssend, obuf, sbuf,
               q_send, q_recv, kv_send, kv_recv, pair_send, pair_recv, o_send, o_recv, s_send, s_recv):
        row, col = lax.axis_index("qrow"), lax.axis_index("kcol")
        group = row // fold
        member = (row % fold) * cols_n + col
        me = row * cols_n + col
        my_block = col * rows_n + row
        my_slot = sum(i * (member == e).astype(jnp.int32) for i, e in enumerate(slots))

        half = lax.rem(member, 2)
        barrier = pltpu.get_barrier_semaphore()

        fetch = pltpu.make_async_copy(kv_ref, local, local_sem)
        fetch.start()

        @pl.loop(1, devices)
        def _(k):
            other = lax.rem(me + k, devices)
            pl.semaphore_signal(barrier, inc=1, device_id=(other // cols_n, other % cols_n), device_id_type=MESH)

        for i, e in enumerate(maybe):
            @pl.when(block_of(e, group) < first_live)
            def _():
                kvbuf[:, len(sure) + i] = jnp.zeros((2, BLOCK, HEAD_WIDTH), kvbuf.dtype)

        for e in range(members):
            for h in range(heads):
                first = (e * heads + h) * HEAD_WIDTH
                wide[e, h * local_rows:(h + 1) * local_rows] = q_ref[:, first:first + HEAD_WIDTH].astype(jnp.float32)
            qsend[e] = wide[e].astype(qsend.dtype)

        fetch.wait()
        pl.semaphore_wait(barrier, devices - 1)

        def kv_part(e):
            first = pl.multiple_of(e * heads // (QUERY_HEADS // KEY_VALUE_HEADS) * HEAD_WIDTH, HEAD_WIDTH)
            return local.at[lax.rem(e, 2), :, pl.ds(first, HEAD_WIDTH)]

        def kv_copy(k):
            e = lax.rem(member + k, members)
            return pltpu.make_async_remote_copy(
                src_ref=kv_part(e), dst_ref=kvbuf.at[lax.rem(e, 2), my_slot], send_sem=kv_send.at[k],
                recv_sem=kv_recv.at[my_slot], device_id=where_is(group, e), device_id_type=MESH)

        @pl.when(my_block >= first_live)
        def _():
            pltpu.make_async_copy(kv_part(member), kvbuf.at[half, my_slot], kv_recv.at[my_slot]).start()
            for k in range(1, members):
                kv_copy(k).start()

        pltpu.make_async_copy(qsend.at[member], qbuf.at[me], q_recv.at[group]).start()

        @pl.loop(1, devices)
        def _(k):
            e = lax.rem(member + k, members)
            pltpu.make_async_remote_copy(
                src_ref=qsend.at[e], dst_ref=qbuf.at[me], send_sem=q_send, recv_sem=q_recv.at[group],
                device_id=where_is(visited(group, k // members), e), device_id_type=MESH).start()

        def pair_copy(i):
            return pltpu.make_async_remote_copy(
                src_ref=kvbuf.at[half, i], dst_ref=kvbuf.at[half, i], send_sem=pair_send.at[i],
                recv_sem=pair_recv.at[i], device_id=(row, col + 1 - 2 * lax.rem(col, 2)), device_id_type=MESH)

        def per_slot(step):
            for i, e in enumerate(slots):
                if e in sure:
                    step(i)
                else:
                    pl.when(block_of(e, group) >= first_live)(lambda: step(i))

        def pass_on(i):
            pltpu.make_async_copy(kvbuf.at[half, i], kvbuf.at[half, i], kv_recv.at[i]).wait()
            pair_copy(i).start()

        per_slot(pass_on)
        per_slot(lambda i: pair_copy(i).wait_recv())

        lane = lax.broadcasted_iota(jnp.int32, (chunk_rows, BLOCK), 1)
        row_index = lax.broadcasted_iota(jnp.int32, (chunk_rows, BLOCK), 0)
        row_query = row_index // slice_rows * local_rows + row_index % local_rows
        offset = (lax.broadcasted_iota(jnp.int32, (slice_rows, BLOCK), 1)
                  - lax.broadcasted_iota(jnp.int32, (slice_rows, BLOCK), 0))
        top_place, total_place = offset == 0, offset == slice_rows

        def attend(source):
            first = source * members
            mine = qbuf.at[pl.ds(first, members)]
            pltpu.make_async_copy(mine, mine, q_recv.at[source]).wait()
            q = qbuf[pl.ds(first, members)].reshape(chunk_rows, HEAD_WIDTH)
            query_first = source * chunk_queries
            query_block = (query_first // BLOCK + 1) * stripe_blocks - 1
            in_block = row_query + query_first % BLOCK
            query_doc = doc_ref[query_block]
            keys = kvbuf[0].reshape(len(slots) * BLOCK, HEAD_WIDTH)
            values = kvbuf[1].reshape(len(slots) * BLOCK, HEAD_WIDTH)
            scores = dot(q, keys, ((1,), (1,)))
            masked = []
            for i, e in enumerate(slots):
                b = block_of(e, group)
                same = doc_ref[b] == query_doc
                whole = jnp.where(same & (b < query_block), BLOCK, -1)
                causal = jnp.where(same & (b == query_block), 0, -2 * BLOCK)
                limit = jnp.maximum(in_block + causal, whole)
                masked.append(jnp.where(lane <= limit, scores[:, i * BLOCK:(i + 1) * BLOCK], masked_score))
            top = masked[0]
            for s in masked[1:]:
                top = jnp.maximum(top, s)
            top = jnp.maximum(jnp.max(top, axis=1, keepdims=True), 0.5 * masked_score)
            weights = [jnp.exp2((s - top) * scale) for s in masked]
            total = weights[0]
            for p in weights[1:]:
                total = total + p
            total = jnp.sum(total, axis=1, keepdims=True)
            acc = dot(jnp.concatenate([p.astype(jnp.bfloat16) for p in weights], axis=1), values, ((1,), (0,)))
            osend[pl.ds(first, members)] = acc.astype(jnp.bfloat16).reshape(members, slice_rows, HEAD_WIDTH)
            for j in range(members):
                part = slice(j * slice_rows, (j + 1) * slice_rows)
                stats = jnp.where(top_place, top[part], jnp.where(total_place, total[part], 0.0))
                ssend[first + j] = jnp.sum(stats, axis=0, keepdims=True)

        def give(source, j):
            k = source * members + j
            return [
                pltpu.make_async_remote_copy(
                    src_ref=src.at[k], dst_ref=dst.at[group, member], send_sem=sent, recv_sem=got.at[group],
                    device_id=where_is(source, j), device_id_type=MESH)
                for src, dst, sent, got in ((osend, obuf, o_send, o_recv), (ssend, sbuf, s_send, s_recv))
            ]

        @pl.loop(1, groups)
        def _(k):
            source = lax.rem(group + k, groups)
            attend(source)
            for j in range(members):
                for copy in give(source, j):
                    copy.start()

        attend(group)
        pltpu.make_async_copy(osend.at[me], obuf.at[group, member], o_recv.at[group]).start()
        pltpu.make_async_copy(ssend.at[me], sbuf.at[group, member], s_recv.at[group]).start()
        for i in range(1, members):
            for copy in give(group, lax.rem(member + i, members)):
                copy.start()

        for g in range(groups):
            pltpu.make_async_copy(sbuf.at[g], sbuf.at[g], s_recv.at[g]).wait()
            pltpu.make_async_copy(obuf.at[g], obuf.at[g], o_recv.at[g]).wait()

        for e in range(members):
            column = lambda g, place: jnp.sum(jnp.where(place, sbuf[g, e], 0.0), axis=1, keepdims=True)
            tops = [column(g, top_place) for g in range(groups)]
            overall = tops[0]
            for t in tops[1:]:
                overall = jnp.maximum(overall, t)
            merged = weight = None
            for g in range(groups):
                factor = jnp.exp2((tops[g] - overall) * scale)
                term = factor * obuf[g, e].astype(jnp.float32)
                part = factor * column(g, total_place)
                merged = term if merged is None else merged + term
                weight = part if weight is None else weight + part
            wide[e] = merged / weight
            for h in range(heads):
                first = (e * heads + h) * HEAD_WIDTH
                out_ref[:, first:first + HEAD_WIDTH] = wide[e, h * local_rows:(h + 1) * local_rows].astype(out_ref.dtype)

        per_slot(lambda i: pair_copy(i).wait_send())

        @pl.when(my_block >= first_live)
        def _():
            for k in range(1, members):
                kv_copy(k).wait_send()
        others = qbuf.at[pl.ds(0, devices - 1)]
        pltpu.make_async_copy(others, others, q_send).wait()
        others = osend.at[pl.ds(0, devices - 1)]
        pltpu.make_async_copy(others, others, o_send).wait()
        others = ssend.at[pl.ds(0, devices - 1)]
        pltpu.make_async_copy(others, others, s_send).wait()

    bf16, dma = jnp.bfloat16, pltpu.SemaphoreType.DMA
    scratch = [
        pltpu.VMEM((2, BLOCK, KEY_VALUE_HEADS * HEAD_WIDTH), bf16),
        dma,
        pltpu.VMEM((members, slice_rows, HEAD_WIDTH), bf16),
        pltpu.VMEM((members, slice_rows, HEAD_WIDTH), jnp.float32),
        pltpu.VMEM((devices, slice_rows, HEAD_WIDTH), bf16),
        pltpu.VMEM((2, len(slots), BLOCK, HEAD_WIDTH), bf16),
        pltpu.VMEM((devices, slice_rows, HEAD_WIDTH), bf16),
        pltpu.VMEM((devices, 1, BLOCK), jnp.float32),
        pltpu.VMEM((groups, members, slice_rows, HEAD_WIDTH), bf16),
        pltpu.VMEM((groups, members, 1, BLOCK), jnp.float32),
        dma, dma((groups,)), dma((members,)), dma((len(slots),)), dma((len(slots),)), dma((len(slots),)),
        dma, dma((groups,)), dma, dma((groups,)),
    ]
    return kernel, scratch


def solution(mesh):
    rows_n, cols_n = mesh.shape["qrow"], mesh.shape["kcol"]

    def per_device(queries, keys_values, doc_blocks):
        local_rows = queries.shape[0]
        kernel, scratch = make_kernel(rows_n, cols_n, queries.shape[0], doc_blocks.shape[0])
        return pl.pallas_call(
            kernel,
            out_shape=jax.ShapeDtypeStruct(queries.shape, queries.dtype),
            in_specs=[
                pl.BlockSpec(memory_space=pltpu.SMEM),
                pl.BlockSpec(memory_space=pltpu.VMEM),
                pl.BlockSpec(memory_space=pl.ANY),
            ],
            out_specs=pl.BlockSpec(memory_space=pltpu.VMEM),
            scratch_shapes=scratch,
            compiler_params=pltpu.CompilerParams(collective_id=0, has_side_effects=True),
        )(doc_blocks, queries, keys_values)

    return jax.shard_map(
        per_device,
        mesh=mesh,
        in_specs=(P(("qrow", "kcol"), None), P(None, ("kcol", "qrow"), None), P()),
        out_specs=P(("qrow", "kcol"), None),
        check_vma=False,
    )
```

```python
import math

import jax
import jax.numpy as jnp
from jax import lax
from jax.experimental import pallas as pl
from jax.experimental.pallas import tpu as pltpu
from jax.sharding import PartitionSpec as P

QUERY_HEADS = 64
KEY_VALUE_HEADS = 4
HEAD_WIDTH = 128
BLOCK = 128
MESH = pl.DeviceIdType.MESH

masked_score = -1e30


def dot(a, b, dims):
    return lax.dot_general(a, b, (dims, ((), ())), preferred_element_type=jnp.float32)


def make_kernel(rows_n, cols_n, local_rows, blocks_n):
    fold = max(1, 8 // cols_n)
    groups = rows_n // fold
    members = fold * cols_n
    heads = QUERY_HEADS // members
    slice_rows = local_rows * heads
    chunk_rows = members * slice_rows
    devices = rows_n * cols_n
    total_queries = devices * local_rows
    query_blocks = total_queries // BLOCK
    stripe_blocks = blocks_n // query_blocks
    chunk_queries = members * local_rows
    assert BLOCK % chunk_queries == 0 and blocks_n == devices and cols_n % 2 == 0 and 2 * slice_rows <= BLOCK
    first_live = max(0, stripe_blocks - 1 - blocks_n // 2)
    block_of = lambda e, g: (e % cols_n) * rows_n + g * fold + e // cols_n
    spans = [[block_of(e, g) >= first_live for g in range(groups)] for e in range(members)]
    sure = [e for e in range(members) if all(spans[e])]
    maybe = [e for e in range(members) if any(spans[e]) and not all(spans[e])]
    slots = sure + maybe
    scale = math.log2(math.e) / math.sqrt(HEAD_WIDTH)

    apart = max(1, groups // 2)

    def visited(group, k):
        block = group // apart
        far = lax.rem(block + 1, groups // apart) * apart + lax.rem(group + k, apart)
        near = block * apart + lax.rem(group + k - apart, apart)
        return jnp.where(k == 0, group, jnp.where(k <= apart, far, near))

    def where_is(group, member):
        return (group * fold + member // cols_n, member % cols_n)

    def kernel(doc_ref, q_ref, kv_ref, out_ref, local, local_sem, qsend, wide, qbuf, kvbuf, osend, ssend, obuf, sbuf,
               q_send, q_recv, kv_send, kv_recv, pair_send, pair_recv, o_send, o_recv, s_send, s_recv):
        row, col = lax.axis_index("qrow"), lax.axis_index("kcol")
        group = row // fold
        member = (row % fold) * cols_n + col
        me = row * cols_n + col
        my_block = col * rows_n + row
        my_slot = sum(i * (member == e).astype(jnp.int32) for i, e in enumerate(slots))

        half = lax.rem(member, 2)
        barrier = pltpu.get_barrier_semaphore()

        fetch = pltpu.make_async_copy(kv_ref, local, local_sem)
        fetch.start()

        @pl.loop(1, devices)
        def _(k):
            other = lax.rem(me + k, devices)
            pl.semaphore_signal(barrier, inc=1, device_id=(other // cols_n, other % cols_n), device_id_type=MESH)

        for i, e in enumerate(maybe):
            @pl.when(block_of(e, group) < first_live)
            def _():
                kvbuf[:, len(sure) + i] = jnp.zeros((2, BLOCK, HEAD_WIDTH), kvbuf.dtype)

        for e in range(members):
            for h in range(heads):
                first = (e * heads + h) * HEAD_WIDTH
                wide[e, h * local_rows:(h + 1) * local_rows] = q_ref[:, first:first + HEAD_WIDTH].astype(jnp.float32)
            qsend[e] = wide[e].astype(qsend.dtype)

        fetch.wait()
        pl.semaphore_wait(barrier, devices - 1)

        def kv_part(e):
            first = pl.multiple_of(e * heads // (QUERY_HEADS // KEY_VALUE_HEADS) * HEAD_WIDTH, HEAD_WIDTH)
            return local.at[lax.rem(e, 2), :, pl.ds(first, HEAD_WIDTH)]

        def kv_copy(k):
            e = lax.rem(member + k, members)
            return pltpu.make_async_remote_copy(
                src_ref=kv_part(e), dst_ref=kvbuf.at[lax.rem(e, 2), my_slot], send_sem=kv_send.at[k],
                recv_sem=kv_recv.at[my_slot], device_id=where_is(group, e), device_id_type=MESH)

        @pl.when(my_block >= first_live)
        def _():
            pltpu.make_async_copy(kv_part(member), kvbuf.at[half, my_slot], kv_recv.at[my_slot]).start()
            for k in range(1, members):
                kv_copy(k).start()

        pltpu.make_async_copy(qsend.at[member], qbuf.at[me], q_recv.at[group]).start()

        @pl.loop(1, devices)
        def _(k):
            e = lax.rem(member + k, members)
            pltpu.make_async_remote_copy(
                src_ref=qsend.at[e], dst_ref=qbuf.at[me], send_sem=q_send, recv_sem=q_recv.at[group],
                device_id=where_is(visited(group, k // members), e), device_id_type=MESH).start()

        def pair_copy(i):
            return pltpu.make_async_remote_copy(
                src_ref=kvbuf.at[half, i], dst_ref=kvbuf.at[half, i], send_sem=pair_send.at[i],
                recv_sem=pair_recv.at[i], device_id=(row, col + 1 - 2 * lax.rem(col, 2)), device_id_type=MESH)

        def per_slot(step):
            for i, e in enumerate(slots):
                if e in sure:
                    step(i)
                else:
                    pl.when(block_of(e, group) >= first_live)(lambda: step(i))

        def pass_on(i):
            pltpu.make_async_copy(kvbuf.at[half, i], kvbuf.at[half, i], kv_recv.at[i]).wait()
            pair_copy(i).start()

        per_slot(pass_on)
        per_slot(lambda i: pair_copy(i).wait_recv())

        lane = lax.broadcasted_iota(jnp.int32, (chunk_rows, BLOCK), 1)
        row_index = lax.broadcasted_iota(jnp.int32, (chunk_rows, BLOCK), 0)
        row_query = row_index // slice_rows * local_rows + row_index % local_rows
        offset = (lax.broadcasted_iota(jnp.int32, (slice_rows, BLOCK), 1)
                  - lax.broadcasted_iota(jnp.int32, (slice_rows, BLOCK), 0))
        top_place, total_place = offset == 0, offset == slice_rows

        def attend(source):
            first = source * members
            mine = qbuf.at[pl.ds(first, members)]
            pltpu.make_async_copy(mine, mine, q_recv.at[source]).wait()
            q = qbuf[pl.ds(first, members)].reshape(chunk_rows, HEAD_WIDTH)
            query_first = source * chunk_queries
            query_block = (query_first // BLOCK + 1) * stripe_blocks - 1
            in_block = row_query + query_first % BLOCK
            query_doc = doc_ref[query_block]
            keys = kvbuf[0].reshape(len(slots) * BLOCK, HEAD_WIDTH)
            values = kvbuf[1].reshape(len(slots) * BLOCK, HEAD_WIDTH)
            scores = dot(q, keys, ((1,), (1,)))
            masked = []
            for i, e in enumerate(slots):
                b = block_of(e, group)
                same = doc_ref[b] == query_doc
                whole = jnp.where(same & (b < query_block), BLOCK, -1)
                causal = jnp.where(same & (b == query_block), 0, -2 * BLOCK)
                limit = jnp.maximum(in_block + causal, whole)
                masked.append(jnp.where(lane <= limit, scores[:, i * BLOCK:(i + 1) * BLOCK], masked_score))
            top = masked[0]
            for s in masked[1:]:
                top = jnp.maximum(top, s)
            top = jnp.maximum(jnp.max(top, axis=1, keepdims=True), 0.5 * masked_score)
            weights = [jnp.exp2((s - top) * scale) for s in masked]
            total = weights[0]
            for p in weights[1:]:
                total = total + p
            total = jnp.sum(total, axis=1, keepdims=True)
            acc = dot(jnp.concatenate([p.astype(jnp.bfloat16) for p in weights], axis=1), values, ((1,), (0,)))
            osend[pl.ds(first, members)] = acc.astype(jnp.bfloat16).reshape(members, slice_rows, HEAD_WIDTH)
            for j in range(members):
                part = slice(j * slice_rows, (j + 1) * slice_rows)
                stats = jnp.where(top_place, top[part], jnp.where(total_place, total[part], 0.0))
                ssend[first + j] = jnp.sum(stats, axis=0, keepdims=True)

        def give(source, j):
            k = source * members + j
            return [
                pltpu.make_async_remote_copy(
                    src_ref=src.at[k], dst_ref=dst.at[group, member], send_sem=sent, recv_sem=got.at[group],
                    device_id=where_is(source, j), device_id_type=MESH)
                for src, dst, sent, got in ((osend, obuf, o_send, o_recv), (ssend, sbuf, s_send, s_recv))
            ]

        def step(k):
            source = lax.rem(group + k, groups)
            attend(source)
            for j in range(members):
                for copy in give(source, j):
                    copy.start()

        if groups <= 4:
            for k in range(1, groups):
                step(k)
        else:
            pl.loop(1, groups)(step)

        attend(group)
        pltpu.make_async_copy(osend.at[me], obuf.at[group, member], o_recv.at[group]).start()
        pltpu.make_async_copy(ssend.at[me], sbuf.at[group, member], s_recv.at[group]).start()
        for i in range(1, members):
            for copy in give(group, lax.rem(member + i, members)):
                copy.start()

        for g in range(groups):
            pltpu.make_async_copy(sbuf.at[g], sbuf.at[g], s_recv.at[g]).wait()
            pltpu.make_async_copy(obuf.at[g], obuf.at[g], o_recv.at[g]).wait()

        for e in range(members):
            column = lambda g, place: jnp.sum(jnp.where(place, sbuf[g, e], 0.0), axis=1, keepdims=True)
            tops = [column(g, top_place) for g in range(groups)]
            overall = tops[0]
            for t in tops[1:]:
                overall = jnp.maximum(overall, t)
            merged = weight = None
            for g in range(groups):
                factor = jnp.exp2((tops[g] - overall) * scale)
                term = factor * obuf[g, e].astype(jnp.float32)
                part = factor * column(g, total_place)
                merged = term if merged is None else merged + term
                weight = part if weight is None else weight + part
            wide[e] = merged / weight
            for h in range(heads):
                first = (e * heads + h) * HEAD_WIDTH
                out_ref[:, first:first + HEAD_WIDTH] = wide[e, h * local_rows:(h + 1) * local_rows].astype(out_ref.dtype)

        per_slot(lambda i: pair_copy(i).wait_send())

        @pl.when(my_block >= first_live)
        def _():
            for k in range(1, members):
                kv_copy(k).wait_send()
        others = qbuf.at[pl.ds(0, devices - 1)]
        pltpu.make_async_copy(others, others, q_send).wait()
        others = osend.at[pl.ds(0, devices - 1)]
        pltpu.make_async_copy(others, others, o_send).wait()
        others = ssend.at[pl.ds(0, devices - 1)]
        pltpu.make_async_copy(others, others, s_send).wait()

    bf16, dma = jnp.bfloat16, pltpu.SemaphoreType.DMA
    scratch = [
        pltpu.VMEM((2, BLOCK, KEY_VALUE_HEADS * HEAD_WIDTH), bf16),
        dma,
        pltpu.VMEM((members, slice_rows, HEAD_WIDTH), bf16),
        pltpu.VMEM((members, slice_rows, HEAD_WIDTH), jnp.float32),
        pltpu.VMEM((devices, slice_rows, HEAD_WIDTH), bf16),
        pltpu.VMEM((2, len(slots), BLOCK, HEAD_WIDTH), bf16),
        pltpu.VMEM((devices, slice_rows, HEAD_WIDTH), bf16),
        pltpu.VMEM((devices, 1, BLOCK), jnp.float32),
        pltpu.VMEM((groups, members, slice_rows, HEAD_WIDTH), bf16),
        pltpu.VMEM((groups, members, 1, BLOCK), jnp.float32),
        dma, dma((groups,)), dma((members,)), dma((len(slots),)), dma((len(slots),)), dma((len(slots),)),
        dma, dma((groups,)), dma, dma((groups,)),
    ]
    return kernel, scratch


def solution(mesh):
    rows_n, cols_n = mesh.shape["qrow"], mesh.shape["kcol"]

    def per_device(queries, keys_values, doc_blocks):
        local_rows = queries.shape[0]
        kernel, scratch = make_kernel(rows_n, cols_n, queries.shape[0], doc_blocks.shape[0])
        return pl.pallas_call(
            kernel,
            out_shape=jax.ShapeDtypeStruct(queries.shape, queries.dtype),
            in_specs=[
                pl.BlockSpec(memory_space=pltpu.SMEM),
                pl.BlockSpec(memory_space=pltpu.VMEM),
                pl.BlockSpec(memory_space=pl.ANY),
            ],
            out_specs=pl.BlockSpec(memory_space=pltpu.VMEM),
            scratch_shapes=scratch,
            compiler_params=pltpu.CompilerParams(collective_id=0, has_side_effects=True),
        )(doc_blocks, queries, keys_values)

    return jax.shard_map(
        per_device,
        mesh=mesh,
        in_specs=(P(("qrow", "kcol"), None), P(None, ("kcol", "qrow"), None), P()),
        out_specs=P(("qrow", "kcol"), None),
        check_vma=False,
    )
```
